32 devices in a mesh: groups: 2 (over y), wide: 8 (over z, x), head: 2 (over core).
Axes of the slice: x: 2, y: 2, z: 4, core: 2. Of those that a mesh axis runs over, the one named last changes fastest.
Arguments:
- tokens: bfloat16 [1024, 2048], P(('groups', 'wide'), 'head'), parts along dimension 0, may hold values from -6 to 6
- expert_ids: int32 [1024, 8], P(('groups', 'wide')), parts along dimension 0, may hold values from 0 to 7, as said below
- gate_scores: float32 [1024, 8], P(('groups', 'wide')), parts along dimension 0, may hold values from 0.25 to 1
- gate_proj: bfloat16 [8, 704, 2048], P('wide', 'head'), may hold values from -0.125 to 0.125
- up_proj: bfloat16 [8, 704, 2048], P('wide', 'head'), may hold values from -0.125 to 0.125
- down_proj: bfloat16 [8, 704, 2048], P('wide', 'head'), may hold values from -0.21875 to 0.21875
Outputs:
- mixed: bfloat16 [1024, 2048], P(('groups', 'wide'), 'head'), parts along dimension 0
The draws below stay inside these ranges and needn't reach their ends.
There are 2 independent parts, one for each index of `groups`. The reference program is written for one: setup_inputs(seed, part) draws one part's arguments, and reference() takes and returns one part's arrays. A program takes and returns all parts, laid end to end along the dimension named above; an argument that names none is the same for every part. Nothing has to cross between parts.
Inputs may be any that keep to these rules, and one draw needn't show every extreme that they name: `expert_ids`: each row names 8 different experts. Within each aligned block of 64 rows at most 64 rows name the same expert, and in every draw one expert is named by exactly 64 rows of every such block.
All inputs are finite; a program needn't handle non-finite values.
Results may differ from the reference program's by a relative error of at most 0.01.
Values may be sent and summed in bfloat16 or wider, within the bound.
A program may use at most 64 MiB of HBM per device.

```python
import math
import jax
import jax.numpy as jnp
from jax import lax

D = 2048
FF = 704
TOP = 8
TOK_DEV = 64
TOKENS = 512
EXPERTS = 8
CAP = 64
N_WIDE = 8


def draw_expert_ids(key, part):
    block_count = TOKENS // TOK_DEV
    hot_key, pref_key, rows_key = jax.random.split(jax.random.fold_in(key, 7), 3)
    hot_expert = jax.random.randint(hot_key, (), 0, EXPERTS)
    preference = jax.random.randint(pref_key, (EXPERTS,), 0, 2048)
    expert_numbers = jnp.arange(EXPERTS, dtype=jnp.int32)

    def draw_block(block_key):
        row_noise = jax.random.randint(block_key, (TOK_DEV, EXPERTS), 0, 2048)

        def assign_row(counts_now, noise_row):
            scores = preference + noise_row
            boosted = jnp.logical_and(expert_numbers == hot_expert, counts_now < CAP)
            scores = jnp.where(boosted, scores + 8192, scores)
            scores = jnp.where(counts_now >= CAP, -1, scores)
            keyed_scores = scores * EXPERTS + expert_numbers
            unused, chosen = lax.top_k(keyed_scores, TOP)
            chosen = chosen.astype(jnp.int32)
            added = jnp.sum((chosen[:, None] == expert_numbers[None, :]).astype(jnp.int32), axis=0)
            return (counts_now + added, chosen)
        unused, drawn_ids = lax.scan(assign_row, jnp.zeros((EXPERTS,), jnp.int32), row_noise)
        return drawn_ids
    block_keys = jax.random.split(rows_key, block_count)
    drawn_ids = jax.vmap(draw_block)(block_keys)
    return drawn_ids.reshape(TOKENS, TOP).astype(jnp.int32)


def levels(key, extent, shards, low, largest):
    def one(position, blocks):
        steps = jax.random.uniform(jax.random.fold_in(jax.random.fold_in(key, 6), position), (blocks,), jnp.float32, low / len(shards), largest / len(shards))
        return jnp.repeat(jnp.exp(steps), extent[position] // blocks).reshape((-1,) + (1,) * (len(extent) - position - 1))

    level = one(*shards[0])
    for cut in shards[1:]:
        level = level * one(*cut)
    return level


def normal_values(key, shape, spread, reach, cuts=(), kind=jnp.bfloat16):
    result = jax.random.normal(key, shape, jnp.float32) * spread
    if len(cuts) > 0:
        result = levels(key, shape, cuts, -0.22, 0.18) * result
    return jnp.clip(result, min=-reach, max=reach).astype(kind)


def setup_inputs(seed: int = 0, part: int = 0) -> dict:
    key_list = jax.random.split(jax.random.key(seed), 7)
    part_keys = jax.random.split(jax.random.fold_in(key_list[6], part), 7)
    tokens = normal_values(part_keys[0], (TOKENS, D), 1.0, 6.0, ((0, 8), (1, 2)))
    expert_ids = draw_expert_ids(jax.random.fold_in(jax.random.fold_in(key_list[6], part), 71), part)
    gate_scores = jnp.clip(jnp.exp(math.log(1.0) - 1.3862944 * jax.random.uniform(part_keys[2], (TOKENS, TOP), jnp.float32) ** levels(part_keys[2], (TOKENS, TOP), ((0, 8),), -0.2, 0.2)), 0.25, 1.0)
    gate_proj = normal_values(key_list[3], (EXPERTS, FF, D), D ** -0.5, 0.125, ((0, 8), (1, 2)))
    up_proj = normal_values(key_list[4], (EXPERTS, FF, D), D ** -0.5, 0.125, ((0, 8), (1, 2)))
    down_proj = normal_values(key_list[5], (EXPERTS, FF, D), FF ** -0.5, 0.21875, ((0, 8), (1, 2)))
    return {"tokens": tokens, "expert_ids": expert_ids, "gate_scores": gate_scores, "gate_proj": gate_proj, "up_proj": up_proj, "down_proj": down_proj}


def reference(tokens, expert_ids, gate_scores, gate_proj, up_proj, down_proj):
    token_count = tokens.shape[0]
    feature_width = tokens.shape[1]
    half_units = FF // 2
    slot_room = N_WIDE * CAP
    slot_numbers = jnp.arange(slot_room, dtype=jnp.int32)

    def one_expert(running, stacked_in):
        expert, w_gate, w_up, w_down = stacked_in
        chosen = expert_ids == expert
        weight = jnp.sum(jnp.where(chosen, gate_scores, jnp.zeros_like(gate_scores)), axis=1)
        named = jnp.any(chosen, axis=1)
        row_index = jnp.nonzero(named, size=slot_room, fill_value=0)[0].astype(jnp.int32)
        filled = slot_numbers < jnp.sum(named.astype(jnp.int32))
        picked = tokens[row_index]
        gate_part = jnp.dot(picked, w_gate.T, preferred_element_type=jnp.float32)
        up_part = jnp.dot(picked, w_up.T, preferred_element_type=jnp.float32)
        hidden = (jax.nn.silu(gate_part) * up_part).astype(jnp.bfloat16)
        lower_part = jnp.dot(hidden[:, :half_units], w_down[:half_units], preferred_element_type=jnp.float32).astype(jnp.bfloat16)
        upper_part = jnp.dot(hidden[:, half_units:], w_down[half_units:], preferred_element_type=jnp.float32).astype(jnp.bfloat16)
        expert_out = lower_part.astype(jnp.float32) + upper_part.astype(jnp.float32)
        scale_rows = jnp.where(filled, weight[row_index], jnp.zeros_like(weight[row_index]))
        weighted = expert_out * scale_rows[:, None]
        running = running.at[row_index].add(weighted)
        return running, None

    start = jnp.zeros((token_count, feature_width), jnp.float32)
    experts_list = jnp.arange(EXPERTS, dtype=jnp.int32)
    running_sum, unused = lax.scan(one_expert, start, (experts_list, gate_proj, up_proj, down_proj))
    return running_sum.astype(jnp.bfloat16)
```

```python
import functools

import jax
import jax.numpy as jnp
from jax import lax
from jax.experimental import pallas as pl
from jax.experimental.pallas import tpu as pltpu
from jax.sharding import PartitionSpec as P


def spread(tokens, expert_ids, gate_scores, gate_proj, up_proj, down_proj):
    experts = lax.axis_size("wide")
    tok_rows, top_count = expert_ids.shape
    ceiling = (tok_rows * top_count + experts - 1) // experts
    capacity = min(tok_rows, max(2, tok_rows // 8, 2 * ceiling))
    flat_ids = expert_ids.reshape(-1)
    expert_numbers = jnp.arange(experts, dtype=jnp.int32)
    onehot = (flat_ids[:, None] == expert_numbers[None, :]).astype(jnp.int32)
    earlier = jnp.cumsum(onehot, axis=0) - onehot
    slot_index = jnp.sum(earlier * onehot, axis=1)
    position = flat_ids * capacity + slot_index
    targets = jnp.arange(experts * capacity, dtype=jnp.int32)
    placing = jnp.any(
        position.reshape(tok_rows, top_count)[:, :, None] == targets[None, None, :], axis=1
    ).astype(jnp.bfloat16)
    w_gate = gate_proj[0]
    w_up = up_proj[0]
    w_down = down_proj[0]
    placed = lax.dot_general(
        placing, tokens, (((0,), (0,)), ((), ())), preferred_element_type=jnp.float32
    )
    outgoing = placed.astype(jnp.bfloat16).reshape(experts, capacity, tokens.shape[1])
    full_rows = lax.all_gather(
        lax.all_to_all(outgoing, "wide", split_axis=0, concat_axis=0, tiled=True),
        "head",
        axis=2,
        tiled=True,
    )
    src_count, item_count, feature_width = full_rows.shape
    stacked = full_rows.reshape(src_count * item_count, feature_width)
    gate_part = lax.dot_general(
        stacked, w_gate, (((1,), (1,)), ((), ())), preferred_element_type=jnp.float32
    )
    up_part = lax.dot_general(
        stacked, w_up, (((1,), (1,)), ((), ())), preferred_element_type=jnp.float32
    )
    hidden = (jax.nn.silu(gate_part) * up_part).astype(jnp.bfloat16)
    partial_value = jnp.dot(hidden, w_down, preferred_element_type=jnp.float32)
    partial_value = partial_value.reshape(src_count, item_count, feature_width)
    back = lax.psum_scatter(
        partial_value.astype(jnp.bfloat16), "head", scatter_dimension=2, tiled=True
    ).astype(jnp.float32)
    returned = lax.all_to_all(
        back.astype(jnp.bfloat16), "wide", split_axis=0, concat_axis=0, tiled=True
    ).astype(back.dtype)
    picked = returned.reshape(experts * capacity, returned.shape[2])[position]
    picked = picked.reshape(tok_rows, top_count, returned.shape[2])
    mixed = jnp.sum(gate_scores[:, :, None] * picked, axis=1)
    return mixed.astype(jnp.bfloat16)


MESH = pl.DeviceIdType.MESH


def kernel(
    lines, tokens, ids, scores, gate_hbm, up_hbm, down_hbm, out,
    w_gate, w_up, w_down, toks, wt_out, wt_in, hb_out, hb_in, own, xb_out, xb_in,
    zb_out, zb_in, load_sem, swt, rwt, sz, rz, sx, rx, sh, rh, shb, rhb, sxb, rxb, szb, rzb,
):
    wide = lax.axis_index("wide")
    head = lax.axis_index("head")
    line = wide // 2
    side = wide % 2
    far_side = 1 - side
    other = 1 - head
    rows, width = tokens.shape
    experts = 2 * lines

    def at(line_to, side_to, head_to):
        return {"wide": line_to * 2 + side_to, "head": head_to}

    def rcopy(src, dst, ssem, rsem, target):
        return pltpu.make_async_remote_copy(
            src_ref=src, dst_ref=dst, send_sem=ssem, recv_sem=rsem,
            device_id=target, device_id_type=MESH,
        )

    partner = at(line, side, other)
    across = at(line, far_side, head)

    loads = [
        pltpu.make_async_copy(gate_hbm.at[0], w_gate, load_sem.at[0]),
        pltpu.make_async_copy(up_hbm.at[0], w_up, load_sem.at[1]),
        pltpu.make_async_copy(down_hbm.at[0], w_down, load_sem.at[2]),
    ]
    for c in loads:
        c.start()

    barrier = pltpu.get_barrier_semaphore()
    for step in range(1, experts):
        pl.semaphore_signal(
            barrier, inc=1, device_id={"wide": (wide + step) % experts, "head": head},
            device_id_type=MESH,
        )
    pl.semaphore_signal(barrier, inc=1, device_id=partner, device_id_type=MESH)

    lanes = lax.broadcasted_iota(jnp.int32, (rows, 128), 1)
    weight = jnp.zeros((rows, 128), jnp.float32)
    for k in range(ids.shape[1]):
        weight += jnp.where(lanes == ids[:, k : k + 1], scores[:, k : k + 1], 0.0)
    padded = jnp.concatenate([weight, jnp.zeros((128 - rows, 128), jnp.float32)], axis=0)
    turned = jnp.transpose(padded)[:experts]
    wt_out[...] = turned
    wt_in[wide] = turned
    toks[line, side, head] = tokens[...]
    pl.semaphore_wait(barrier, experts)

    def z_send(step):
        dest = (line + step) % lines
        return rcopy(
            tokens, toks.at[line, side, head], sz.at[dest], rz.at[line], at(dest, side, head)
        )

    def x_send(pos):
        return rcopy(
            toks.at[pos, side, head], toks.at[pos, side, head], sx.at[pos], rx.at[pos], across
        )

    def h_send(pos, sd):
        return rcopy(
            toks.at[pos, sd, head], toks.at[pos, sd, head], sh.at[pos, sd], rh.at[pos, sd], partner
        )

    def own_x():
        return rcopy(tokens, toks.at[line, side, head], sx.at[line], rx.at[line], across)

    def own_h():
        return rcopy(
            tokens, toks.at[line, side, head], sh.at[line, side], rh.at[line, side], partner
        )

    low = jnp.minimum(line, lines - 1 - line)
    up_is_long = line < lines - 1 - line

    def order(j):
        d = (j + 1) // 2
        near = line - d if j % 2 else line + d
        return jnp.where(j <= 2 * low, near, jnp.where(up_is_long, j, lines - 1 - j))

    places = [line] + [order(j) for j in range(1, lines)]

    def z_to(dest):
        return rcopy(
            tokens, toks.at[line, side, head], sz.at[dest], rz.at[line], at(dest, side, head)
        )

    def wt_send(step):
        return rcopy(
            wt_out, wt_in.at[wide], swt.at[step], rwt.at[step],
            {"wide": (wide + step) % experts, "head": head},
        )

    own_x().start()
    for j in range(1, lines):
        z_to(places[j]).start()
    own_h().start()
    for step in range(1, experts):
        wt_send(step).start()

    def z_arrive(j):
        pos = places[j]
        rcopy(tokens, toks.at[pos, side, head], sz.at[pos], rz.at[pos], across).wait_recv()
        x_send(pos).start()
        h_send(pos, side).start()

    def x_arrive(j):
        pos = places[j]
        rcopy(
            tokens, toks.at[pos, far_side, head], sx.at[pos], rx.at[pos], across
        ).wait_recv()
        h_send(pos, far_side).start()

    mine = lax.broadcasted_iota(jnp.int32, (128, experts), 1) == wide

    def column(sender):
        return jnp.sum(
            jnp.where(mine, jnp.transpose(wt_in[sender]), 0.0), axis=1, keepdims=True
        )[:rows]

    nt = (((1,), (1,)), ((), ()))

    def compute(j):
        pos = places[j]
        for sd in range(2):
            rcopy(
                tokens, toks.at[pos, sd, other], sh.at[pos, sd], rh.at[pos, sd], partner
            ).wait_recv()
        if j == 0:
            for step in range(1, experts):
                wt_send(step).wait_recv()
            loads[0].wait()
            loads[1].wait()
        gate = jnp.zeros((2 * rows, w_gate.shape[0]), jnp.float32)
        up = gate
        for hf in range(2):
            block = toks[pos, :, hf].reshape(2 * rows, width)
            span = slice(hf * width, (hf + 1) * width)
            gate += lax.dot_general(block, w_gate[:, span], nt, preferred_element_type=jnp.float32)
            up += lax.dot_general(block, w_up[:, span], nt, preferred_element_type=jnp.float32)
        scale = jnp.concatenate([column(pos * 2), column(pos * 2 + 1)], axis=0)
        hidden = (gate / (1.0 + jnp.exp(-gate)) * up * scale).astype(jnp.bfloat16)
        if j == 0:
            loads[2].wait()
        theirs = pl.ds(pl.multiple_of(other * width, width), width)
        part = jnp.dot(hidden, w_down[:, theirs], preferred_element_type=jnp.float32)
        hb_out[pos] = part.astype(jnp.bfloat16).reshape(2, rows, width)
        hb(pos).start()
        ours = pl.ds(pl.multiple_of(head * width, width), width)
        part = jnp.dot(hidden, w_down[:, ours], preferred_element_type=jnp.float32)
        own[j] = part.reshape(2, rows, width)

    def hb(pos):
        return rcopy(hb_out.at[pos], hb_in.at[pos], shb.at[pos], rhb.at[pos], partner)

    def xb(pos):
        return rcopy(xb_out.at[pos], xb_in.at[pos], sxb.at[pos], rxb.at[pos], across)

    def zb(pos):
        return rcopy(
            zb_out.at[pos], zb_in.at[line], szb.at[pos], rzb.at[line], at(pos, side, head)
        )

    def add_heads(j):
        pos = places[j]
        hb(pos).wait_recv()
        xb_out[pos] = (
            own[j, far_side] + hb_in[pos, far_side].astype(jnp.float32)
        ).astype(jnp.bfloat16)
        xb(pos).start()

    def add_sides(j):
        pos = places[j]
        xb(pos).wait_recv()
        total = (
            own[j, side] + hb_in[pos, side].astype(jnp.float32)
            + xb_in[pos].astype(jnp.float32)
        )
        if j == 0:
            own[0, side] = total
        else:
            zb_out[pos] = total.astype(jnp.bfloat16)
            zb(pos).start()

    x_arrive(0)
    for j in range(lines):
        if j + 1 < lines:
            z_arrive(j + 1)
        compute(j)
        if j + 1 < lines:
            x_arrive(j + 1)
        add_heads(j)
        if j > 0:
            add_sides(j - 1)
    add_sides(lines - 1)
    total = own[0, side]
    for j in range(1, lines):
        pos = places[j]
        rcopy(
            zb_out.at[pos], zb_in.at[pos], szb.at[pos], rzb.at[pos], across
        ).wait_recv()
        total += zb_in[pos].astype(jnp.float32)
    out[...] = total.astype(jnp.bfloat16)

    for step in range(1, experts):
        wt_send(step).wait_send()
    own_x().wait_send()
    own_h().wait_send()
    for j in range(1, lines):
        pos = places[j]
        z_to(pos).wait_send()
        x_send(pos).wait_send()
        h_send(pos, side).wait_send()
        zb(pos).wait_send()
    for j in range(lines):
        pos = places[j]
        h_send(pos, far_side).wait_send()
        hb(pos).wait_send()
        xb(pos).wait_send()


def fused(tokens, expert_ids, gate_scores, gate_proj, up_proj, down_proj):
    experts = lax.axis_size("wide")
    lines = experts // 2
    rows, width = tokens.shape
    units, features = gate_proj.shape[1:]
    bf16, f32 = jnp.bfloat16, jnp.float32
    dma = pltpu.SemaphoreType.DMA
    vmem = pl.BlockSpec(memory_space=pltpu.VMEM)
    hbm = pl.BlockSpec(memory_space=pl.ANY)
    return pl.pallas_call(
        functools.partial(kernel, lines),
        out_shape=jax.ShapeDtypeStruct((rows, width), bf16),
        in_specs=[vmem, vmem, vmem, hbm, hbm, hbm],
        out_specs=vmem,
        scratch_shapes=[
            pltpu.VMEM((units, features), bf16),
            pltpu.VMEM((units, features), bf16),
            pltpu.VMEM((units, features), bf16),
            pltpu.VMEM((lines, 2, 2, rows, width), bf16),
            pltpu.VMEM((experts, 128), f32),
            pltpu.VMEM((experts, experts, 128), f32),
            pltpu.VMEM((lines, 2, rows, width), bf16),
            pltpu.VMEM((lines, 2, rows, width), bf16),
            pltpu.VMEM((lines, 2, rows, width), f32),
            pltpu.VMEM((lines, rows, width), bf16),
            pltpu.VMEM((lines, rows, width), bf16),
            pltpu.VMEM((lines, rows, width), bf16),
            pltpu.VMEM((lines, rows, width), bf16),
            dma((3,)),
            dma((experts,)), dma((experts,)),
            dma((lines,)), dma((lines,)),
            dma((lines,)), dma((lines,)),
            dma((lines, 2)), dma((lines, 2)),
            dma((lines,)), dma((lines,)),
            dma((lines,)), dma((lines,)),
            dma((lines,)), dma((lines,)),
        ],
        compiler_params=pltpu.CompilerParams(
            collective_id=0, has_side_effects=True, vmem_limit_bytes=48 * 1024 * 1024
        ),
    )(tokens, expert_ids, gate_scores, gate_proj, up_proj, down_proj)


def local(tokens, expert_ids, gate_scores, gate_proj, up_proj, down_proj):
    experts = lax.axis_size("wide")
    rows, width = tokens.shape
    everyone = expert_ids.shape[1] == experts and gate_proj.shape[0] == 1
    if everyone and experts % 2 == 0 and rows <= 128 and gate_proj.shape[2] == 2 * width:
        return fused(tokens, expert_ids, gate_scores, gate_proj, up_proj, down_proj)
    return spread(tokens, expert_ids, gate_scores, gate_proj, up_proj, down_proj)


def solution(mesh):
    return jax.shard_map(
        local,
        mesh=mesh,
        in_specs=(
            P(("groups", "wide"), "head"),
            P(("groups", "wide"), None),
            P(("groups", "wide"), None),
            P("wide", "head", None),
            P("wide", "head", None),
            P("wide", "head", None),
        ),
        out_specs=P(("groups", "wide"), "head"),
        check_vma=False,
    )
```

```python
import functools

import jax
import jax.numpy as jnp
from jax import lax
from jax.experimental import pallas as pl
from jax.experimental.pallas import tpu as pltpu
from jax.sharding import PartitionSpec as P


def spread(tokens, expert_ids, gate_scores, gate_proj, up_proj, down_proj):
    experts = lax.axis_size("wide")
    tok_rows, top_count = expert_ids.shape
    ceiling = (tok_rows * top_count + experts - 1) // experts
    capacity = min(tok_rows, max(2, tok_rows // 8, 2 * ceiling))
    flat_ids = expert_ids.reshape(-1)
    expert_numbers = jnp.arange(experts, dtype=jnp.int32)
    onehot = (flat_ids[:, None] == expert_numbers[None, :]).astype(jnp.int32)
    earlier = jnp.cumsum(onehot, axis=0) - onehot
    slot_index = jnp.sum(earlier * onehot, axis=1)
    position = flat_ids * capacity + slot_index
    targets = jnp.arange(experts * capacity, dtype=jnp.int32)
    placing = jnp.any(
        position.reshape(tok_rows, top_count)[:, :, None] == targets[None, None, :], axis=1
    ).astype(jnp.bfloat16)
    w_gate = gate_proj[0]
    w_up = up_proj[0]
    w_down = down_proj[0]
    placed = lax.dot_general(
        placing, tokens, (((0,), (0,)), ((), ())), preferred_element_type=jnp.float32
    )
    outgoing = placed.astype(jnp.bfloat16).reshape(experts, capacity, tokens.shape[1])
    full_rows = lax.all_gather(
        lax.all_to_all(outgoing, "wide", split_axis=0, concat_axis=0, tiled=True),
        "head",
        axis=2,
        tiled=True,
    )
    src_count, item_count, feature_width = full_rows.shape
    stacked = full_rows.reshape(src_count * item_count, feature_width)
    gate_part = lax.dot_general(
        stacked, w_gate, (((1,), (1,)), ((), ())), preferred_element_type=jnp.float32
    )
    up_part = lax.dot_general(
        stacked, w_up, (((1,), (1,)), ((), ())), preferred_element_type=jnp.float32
    )
    hidden = (jax.nn.silu(gate_part) * up_part).astype(jnp.bfloat16)
    partial_value = jnp.dot(hidden, w_down, preferred_element_type=jnp.float32)
    partial_value = partial_value.reshape(src_count, item_count, feature_width)
    back = lax.psum_scatter(
        partial_value.astype(jnp.bfloat16), "head", scatter_dimension=2, tiled=True
    ).astype(jnp.float32)
    returned = lax.all_to_all(
        back.astype(jnp.bfloat16), "wide", split_axis=0, concat_axis=0, tiled=True
    ).astype(back.dtype)
    picked = returned.reshape(experts * capacity, returned.shape[2])[position]
    picked = picked.reshape(tok_rows, top_count, returned.shape[2])
    mixed = jnp.sum(gate_scores[:, :, None] * picked, axis=1)
    return mixed.astype(jnp.bfloat16)


MESH = pl.DeviceIdType.MESH


def kernel(
    lines, tok_hbm, ids, scores, gate_hbm, up_hbm, down_hbm, out,
    tokens, w_gate, w_up, w_down, toks, wt_out, wt_in, hb_out, hb_in, own, xb_out, xb_in,
    zb_out, zb_in, load_sem, swt, rwt, sz, rz, sx, rx, sh, rh, shb, rhb, sxb, rxb, szb, rzb,
):
    wide = lax.axis_index("wide")
    head = lax.axis_index("head")
    line = wide // 2
    side = wide % 2
    far_side = 1 - side
    other = 1 - head
    rows, width = tokens.shape
    experts = 2 * lines

    def at(line_to, side_to, head_to):
        return {"wide": line_to * 2 + side_to, "head": head_to}

    def rcopy(src, dst, ssem, rsem, target):
        return pltpu.make_async_remote_copy(
            src_ref=src, dst_ref=dst, send_sem=ssem, recv_sem=rsem,
            device_id=target, device_id_type=MESH,
        )

    partner = at(line, side, other)
    across = at(line, far_side, head)

    token_load = pltpu.make_async_copy(tok_hbm, tokens, load_sem.at[3])
    token_load.start()
    loads = [
        pltpu.make_async_copy(gate_hbm.at[0], w_gate, load_sem.at[0]),
        pltpu.make_async_copy(up_hbm.at[0], w_up, load_sem.at[1]),
        pltpu.make_async_copy(down_hbm.at[0], w_down, load_sem.at[2]),
    ]
    for c in loads:
        c.start()

    barrier = pltpu.get_barrier_semaphore()
    for step in range(1, experts):
        pl.semaphore_signal(
            barrier, inc=1, device_id={"wide": (wide + step) % experts, "head": head},
            device_id_type=MESH,
        )
    pl.semaphore_signal(barrier, inc=1, device_id=partner, device_id_type=MESH)

    named = lax.broadcasted_iota(jnp.int32, (experts, rows), 0)
    turned = jnp.zeros((experts, rows), jnp.float32)
    for k in range(ids.shape[0]):
        turned += jnp.where(named == ids[k : k + 1], scores[k : k + 1], 0.0)
    turned = jnp.concatenate([turned, jnp.zeros((experts, 128 - rows), jnp.float32)], axis=1)
    wt_out[...] = turned
    wt_in[wide] = turned
    token_load.wait()
    toks[line, side, head] = tokens[...]
    pl.semaphore_wait(barrier, experts)

    def x_send(pos):
        return rcopy(
            toks.at[pos, side, head], toks.at[pos, side, head], sx.at[pos], rx.at[pos], across
        )

    def h_send(pos, sd):
        return rcopy(
            toks.at[pos, sd, head], toks.at[pos, sd, head], sh.at[pos, sd], rh.at[pos, sd], partner
        )

    def own_x():
        return rcopy(tokens, toks.at[line, side, head], sx.at[line], rx.at[line], across)

    def own_h():
        return rcopy(
            tokens, toks.at[line, side, head], sh.at[line, side], rh.at[line, side], partner
        )

    low = jnp.minimum(line, lines - 1 - line)
    up_is_long = line < lines - 1 - line

    def order(j):
        d = (j + 1) // 2
        near = line - d if j % 2 else line + d
        return jnp.where(j <= 2 * low, near, jnp.where(up_is_long, j, lines - 1 - j))

    places = [line] + [order(j) for j in range(1, lines)]

    def z_to(dest):
        return rcopy(
            tokens, toks.at[line, side, head], sz.at[dest], rz.at[line], at(dest, side, head)
        )

    def wt_send(step):
        return rcopy(
            wt_out, wt_in.at[wide], swt.at[step], rwt.at[step],
            {"wide": (wide + step) % experts, "head": head},
        )

    own_x().start()
    for j in range(1, lines):
        z_to(places[j]).start()
    own_h().start()
    for step in range(1, experts):
        wt_send(step).start()

    def z_arrive(j):
        pos = places[j]
        rcopy(tokens, toks.at[pos, side, head], sz.at[pos], rz.at[pos], across).wait_recv()
        x_send(pos).start()
        h_send(pos, side).start()

    def x_arrive(j):
        pos = places[j]
        rcopy(
            tokens, toks.at[pos, far_side, head], sx.at[pos], rx.at[pos], across
        ).wait_recv()
        h_send(pos, far_side).start()

    mine = lax.broadcasted_iota(jnp.int32, (128, experts), 1) == wide

    def column(sender):
        return jnp.sum(
            jnp.where(mine, jnp.transpose(wt_in[sender]), 0.0), axis=1, keepdims=True
        )[:rows]

    nt = (((1,), (1,)), ((), ()))

    def compute(j):
        pos = places[j]
        for sd in range(2):
            rcopy(
                tokens, toks.at[pos, sd, other], sh.at[pos, sd], rh.at[pos, sd], partner
            ).wait_recv()
        if j == 0:
            for step in range(1, experts):
                wt_send(step).wait_recv()
            loads[0].wait()
            loads[1].wait()
        gate = jnp.zeros((2 * rows, w_gate.shape[0]), jnp.float32)
        up = gate
        for hf in range(2):
            block = toks[pos, :, hf].reshape(2 * rows, width)
            span = slice(hf * width, (hf + 1) * width)
            gate += lax.dot_general(block, w_gate[:, span], nt, preferred_element_type=jnp.float32)
            up += lax.dot_general(block, w_up[:, span], nt, preferred_element_type=jnp.float32)
        scale = jnp.concatenate([column(pos * 2), column(pos * 2 + 1)], axis=0)
        hidden = (gate / (1.0 + jnp.exp(-gate)) * up * scale).astype(jnp.bfloat16)
        if j == 0:
            loads[2].wait()
        theirs = pl.ds(pl.multiple_of(other * width, width), width)
        part = jnp.dot(hidden, w_down[:, theirs], preferred_element_type=jnp.float32)
        hb_out[pos] = part.astype(jnp.bfloat16).reshape(2, rows, width)
        hb(pos).start()
        ours = pl.ds(pl.multiple_of(head * width, width), width)
        part = jnp.dot(hidden, w_down[:, ours], preferred_element_type=jnp.float32)
        own[j] = part.reshape(2, rows, width)

    def hb(pos):
        return rcopy(hb_out.at[pos], hb_in.at[pos], shb.at[pos], rhb.at[pos], partner)

    def xb(pos):
        return rcopy(xb_out.at[pos], xb_in.at[pos], sxb.at[pos], rxb.at[pos], across)

    def zb(pos):
        return rcopy(
            zb_out.at[pos], zb_in.at[line], szb.at[pos], rzb.at[line], at(pos, side, head)
        )

    def add_heads(j):
        pos = places[j]
        hb(pos).wait_recv()
        xb_out[pos] = (
            own[j, far_side] + hb_in[pos, far_side].astype(jnp.float32)
        ).astype(jnp.bfloat16)
        xb(pos).start()

    def add_sides(j):
        pos = places[j]
        xb(pos).wait_recv()
        total = (
            own[j, side] + hb_in[pos, side].astype(jnp.float32)
            + xb_in[pos].astype(jnp.float32)
        )
        if j == 0:
            own[0, side] = total
        else:
            zb_out[pos] = total.astype(jnp.bfloat16)
            zb(pos).start()

    x_arrive(0)
    for j in range(lines):
        if j + 1 < lines:
            z_arrive(j + 1)
        compute(j)
        if j + 1 < lines:
            x_arrive(j + 1)
        add_heads(j)
        if j > 0:
            add_sides(j - 1)
    add_sides(lines - 1)
    total = own[0, side]
    for j in range(1, lines):
        pos = places[j]
        rcopy(
            zb_out.at[pos], zb_in.at[pos], szb.at[pos], rzb.at[pos], across
        ).wait_recv()
        total += zb_in[pos].astype(jnp.float32)
    out[...] = total.astype(jnp.bfloat16)

    for step in range(1, experts):
        wt_send(step).wait_send()
    own_x().wait_send()
    own_h().wait_send()
    for j in range(1, lines):
        pos = places[j]
        z_to(pos).wait_send()
        x_send(pos).wait_send()
        h_send(pos, side).wait_send()
        zb(pos).wait_send()
    for j in range(lines):
        pos = places[j]
        h_send(pos, far_side).wait_send()
        hb(pos).wait_send()
        xb(pos).wait_send()


def fused(tokens, expert_ids, gate_scores, gate_proj, up_proj, down_proj):
    experts = lax.axis_size("wide")
    lines = experts // 2
    rows, width = tokens.shape
    units, features = gate_proj.shape[1:]
    bf16, f32 = jnp.bfloat16, jnp.float32
    dma = pltpu.SemaphoreType.DMA
    vmem = pl.BlockSpec(memory_space=pltpu.VMEM)
    hbm = pl.BlockSpec(memory_space=pltpu.HBM)
    return pl.pallas_call(
        functools.partial(kernel, lines),
        out_shape=jax.ShapeDtypeStruct((rows, width), bf16),
        in_specs=[hbm, vmem, vmem, hbm, hbm, hbm],
        out_specs=vmem,
        scratch_shapes=[
            pltpu.VMEM((rows, width), bf16),
            pltpu.VMEM((units, features), bf16),
            pltpu.VMEM((units, features), bf16),
            pltpu.VMEM((units, features), bf16),
            pltpu.VMEM((lines, 2, 2, rows, width), bf16),
            pltpu.VMEM((experts, 128), f32),
            pltpu.VMEM((experts, experts, 128), f32),
            pltpu.VMEM((lines, 2, rows, width), bf16),
            pltpu.VMEM((lines, 2, rows, width), bf16),
            pltpu.VMEM((lines, 2, rows, width), f32),
            pltpu.VMEM((lines, rows, width), bf16),
            pltpu.VMEM((lines, rows, width), bf16),
            pltpu.VMEM((lines, rows, width), bf16),
            pltpu.VMEM((lines, rows, width), bf16),
            dma((4,)),
            dma((experts,)), dma((experts,)),
            dma((lines,)), dma((lines,)),
            dma((lines,)), dma((lines,)),
            dma((lines, 2)), dma((lines, 2)),
            dma((lines,)), dma((lines,)),
            dma((lines,)), dma((lines,)),
            dma((lines,)), dma((lines,)),
        ],
        compiler_params=pltpu.CompilerParams(
            collective_id=0, has_side_effects=True, vmem_limit_bytes=63 * 1024 * 1024
        ),
    )(tokens, expert_ids.T, gate_scores.T, gate_proj, up_proj, down_proj)


def local(tokens, expert_ids, gate_scores, gate_proj, up_proj, down_proj):
    experts = lax.axis_size("wide")
    rows, width = tokens.shape
    everyone = expert_ids.shape[1] == experts and gate_proj.shape[0] == 1
    if everyone and experts % 2 == 0 and rows <= 128 and gate_proj.shape[2] == 2 * width:
        return fused(tokens, expert_ids, gate_scores, gate_proj, up_proj, down_proj)
    return spread(tokens, expert_ids, gate_scores, gate_proj, up_proj, down_proj)


def solution(mesh):
    return jax.shard_map(
        local,
        mesh=mesh,
        in_specs=(
            P(("groups", "wide"), "head"),
            P(("groups", "wide"), None),
            P(("groups", "wide"), None),
            P("wide", "head", None),
            P("wide", "head", None),
            P("wide", "head", None),
        ),
        out_specs=P(("groups", "wide"), "head"),
        check_vma=False,
    )
```

```python
import functools

import jax
import jax.numpy as jnp
from jax import lax
from jax.experimental import pallas as pl
from jax.experimental.pallas import tpu as pltpu
from jax.sharding import PartitionSpec as P


def spread(tokens, expert_ids, gate_scores, gate_proj, up_proj, down_proj):
    experts = lax.axis_size("wide")
    tok_rows, top_count = expert_ids.shape
    ceiling = (tok_rows * top_count + experts - 1) // experts
    capacity = min(tok_rows, max(2, tok_rows // 8, 2 * ceiling))
    flat_ids = expert_ids.reshape(-1)
    expert_numbers = jnp.arange(experts, dtype=jnp.int32)
    onehot = (flat_ids[:, None] == expert_numbers[None, :]).astype(jnp.int32)
    earlier = jnp.cumsum(onehot, axis=0) - onehot
    slot_index = jnp.sum(earlier * onehot, axis=1)
    position = flat_ids * capacity + slot_index
    targets = jnp.arange(experts * capacity, dtype=jnp.int32)
    placing = jnp.any(
        position.reshape(tok_rows, top_count)[:, :, None] == targets[None, None, :], axis=1
    ).astype(jnp.bfloat16)
    w_gate = gate_proj[0]
    w_up = up_proj[0]
    w_down = down_proj[0]
    placed = lax.dot_general(
        placing, tokens, (((0,), (0,)), ((), ())), preferred_element_type=jnp.float32
    )
    outgoing = placed.astype(jnp.bfloat16).reshape(experts, capacity, tokens.shape[1])
    full_rows = lax.all_gather(
        lax.all_to_all(outgoing, "wide", split_axis=0, concat_axis=0, tiled=True),
        "head",
        axis=2,
        tiled=True,
    )
    src_count, item_count, feature_width = full_rows.shape
    stacked = full_rows.reshape(src_count * item_count, feature_width)
    gate_part = lax.dot_general(
        stacked, w_gate, (((1,), (1,)), ((), ())), preferred_element_type=jnp.float32
    )
    up_part = lax.dot_general(
        stacked, w_up, (((1,), (1,)), ((), ())), preferred_element_type=jnp.float32
    )
    hidden = (jax.nn.silu(gate_part) * up_part).astype(jnp.bfloat16)
    partial_value = jnp.dot(hidden, w_down, preferred_element_type=jnp.float32)
    partial_value = partial_value.reshape(src_count, item_count, feature_width)
    back = lax.psum_scatter(
        partial_value.astype(jnp.bfloat16), "head", scatter_dimension=2, tiled=True
    ).astype(jnp.float32)
    returned = lax.all_to_all(
        back.astype(jnp.bfloat16), "wide", split_axis=0, concat_axis=0, tiled=True
    ).astype(back.dtype)
    picked = returned.reshape(experts * capacity, returned.shape[2])[position]
    picked = picked.reshape(tok_rows, top_count, returned.shape[2])
    mixed = jnp.sum(gate_scores[:, :, None] * picked, axis=1)
    return mixed.astype(jnp.bfloat16)


MESH = pl.DeviceIdType.MESH
CHUNKS = 2


def kernel(
    lines, tok_hbm, ids, scores, gate_hbm, up_hbm, down_hbm, out,
    tokens, w_gate, w_up, w_down, toks, wt_out, wt_in, hb_out, hb_in, own, xb_out, xb_in,
    zb_out, zb_in, load_sem, swt, rwt, sz, rz, sx, rx, sh, rh, shb, rhb, sxb, rxb, szb, rzb,
):
    wide = lax.axis_index("wide")
    head = lax.axis_index("head")
    line = wide // 2
    side = wide % 2
    far_side = 1 - side
    other = 1 - head
    rows, width = tokens.shape
    experts = 2 * lines

    def at(line_to, side_to, head_to):
        return {"wide": line_to * 2 + side_to, "head": head_to}

    def rcopy(src, dst, ssem, rsem, target):
        return pltpu.make_async_remote_copy(
            src_ref=src, dst_ref=dst, send_sem=ssem, recv_sem=rsem,
            device_id=target, device_id_type=MESH,
        )

    partner = at(line, side, other)
    across = at(line, far_side, head)

    token_load = pltpu.make_async_copy(tok_hbm, tokens, load_sem.at[3])
    token_load.start()
    loads = [
        pltpu.make_async_copy(gate_hbm.at[0], w_gate, load_sem.at[0]),
        pltpu.make_async_copy(up_hbm.at[0], w_up, load_sem.at[1]),
        pltpu.make_async_copy(down_hbm.at[0], w_down, load_sem.at[2]),
    ]
    for c in loads:
        c.start()

    barrier = pltpu.get_barrier_semaphore()
    for step in range(1, experts):
        pl.semaphore_signal(
            barrier, inc=1, device_id={"wide": (wide + step) % experts, "head": head},
            device_id_type=MESH,
        )
    pl.semaphore_signal(barrier, inc=1, device_id=partner, device_id_type=MESH)

    named = lax.broadcasted_iota(jnp.int32, (experts, rows), 0)
    turned = jnp.zeros((experts, rows), jnp.float32)
    for k in range(ids.shape[0]):
        turned += jnp.where(named == ids[k : k + 1], scores[k : k + 1], 0.0)
    turned = jnp.concatenate([turned, jnp.zeros((experts, 128 - rows), jnp.float32)], axis=1)
    wt_out[...] = turned
    wt_in[wide] = turned
    token_load.wait()
    toks[line, side, head] = tokens[...]
    pl.semaphore_wait(barrier, experts)

    chunk = rows // CHUNKS

    def cut(ref, c):
        return ref.at[pl.ds(c * chunk, chunk)]

    def slot(pos, sd, hf, c):
        return toks.at[pos, sd, hf, pl.ds(c * chunk, chunk)]

    def z_send(pos, c, way):
        src = cut(tokens, c) if pos is line else slot(pos, side, head, c)
        to = line + 1 - 2 * way
        return rcopy(
            src, slot(pos, side, head, c), sz.at[pos, c, way], rz.at[pos, c], at(to, side, head)
        )

    def x_send(pos, c):
        src = cut(tokens, c) if pos is line else slot(pos, side, head, c)
        return rcopy(src, slot(pos, side, head, c), sx.at[pos, c], rx.at[pos, c], across)

    def h_send(pos, far, c):
        sd = far_side if far else side
        src = cut(tokens, c) if pos is line and not far else slot(pos, sd, head, c)
        return rcopy(src, slot(pos, sd, head, c), sh.at[pos, sd, c], rh.at[pos, sd, c], partner)

    has_up = line < lines - 1
    has_down = line > 0

    low = jnp.minimum(line, lines - 1 - line)
    up_is_long = line < lines - 1 - line

    def order(j):
        d = (j + 1) // 2
        near = line - d if j % 2 else line + d
        return jnp.where(j <= 2 * low, near, jnp.where(up_is_long, j, lines - 1 - j))

    places = [line] + [order(j) for j in range(1, lines)]

    def wt_send(step):
        return rcopy(
            wt_out, wt_in.at[wide], swt.at[step], rwt.at[step],
            {"wide": (wide + step) % experts, "head": head},
        )

    for c in range(CHUNKS):
        x_send(line, c).start()

        @pl.when(has_up)
        def _():
            z_send(line, c, 0).start()

        @pl.when(has_down)
        def _():
            z_send(line, c, 1).start()

        h_send(line, False, c).start()
    for step in range(1, experts):
        wt_send(step).start()

    def z_arrive(j, c):
        pos = places[j]
        dst = slot(pos, side, head, c)
        rcopy(dst, dst, sz.at[pos, c, 0], rz.at[pos, c], across).wait_recv()

        @pl.when(jnp.logical_and(pos < line, has_up))
        def _():
            z_send(pos, c, 0).start()

        @pl.when(jnp.logical_and(pos > line, has_down))
        def _():
            z_send(pos, c, 1).start()

        x_send(pos, c).start()
        h_send(pos, False, c).start()

    def x_arrive(j, c):
        pos = places[j]
        dst = slot(pos, far_side, head, c)
        rcopy(dst, dst, sx.at[pos, c], rx.at[pos, c], across).wait_recv()
        h_send(pos, True, c).start()

    mine = lax.broadcasted_iota(jnp.int32, (128, experts), 1) == wide

    def column(sender):
        return jnp.sum(
            jnp.where(mine, jnp.transpose(wt_in[sender]), 0.0), axis=1, keepdims=True
        )[:rows]

    nt = (((1,), (1,)), ((), ()))

    def compute(j):
        pos = places[j]
        for sd in range(2):
            for c in range(CHUNKS):
                dst = slot(pos, sd, other, c)
                rcopy(dst, dst, sh.at[pos, sd, c], rh.at[pos, sd, c], partner).wait_recv()
        if j == 0:
            for step in range(1, experts):
                wt_send(step).wait_recv()
            loads[0].wait()
            loads[1].wait()
        gate = jnp.zeros((2 * rows, w_gate.shape[0]), jnp.float32)
        up = gate
        for hf in range(2):
            block = toks[pos, :, hf].reshape(2 * rows, width)
            span = slice(hf * width, (hf + 1) * width)
            gate += lax.dot_general(block, w_gate[:, span], nt, preferred_element_type=jnp.float32)
            up += lax.dot_general(block, w_up[:, span], nt, preferred_element_type=jnp.float32)
        scale = jnp.concatenate([column(pos * 2), column(pos * 2 + 1)], axis=0)
        hidden = (gate / (1.0 + jnp.exp(-gate)) * up * scale).astype(jnp.bfloat16)
        if j == 0:
            loads[2].wait()
        theirs = pl.ds(pl.multiple_of(other * width, width), width)
        part = jnp.dot(hidden, w_down[:, theirs], preferred_element_type=jnp.float32)
        hb_out[pos] = part.astype(jnp.bfloat16).reshape(2, rows, width)
        hb(pos).start()
        ours = pl.ds(pl.multiple_of(head * width, width), width)
        part = jnp.dot(hidden, w_down[:, ours], preferred_element_type=jnp.float32)
        own[j] = part.reshape(2, rows, width)

    def hb(pos):
        return rcopy(hb_out.at[pos], hb_in.at[pos], shb.at[pos], rhb.at[pos], partner)

    def xb(pos):
        return rcopy(xb_out.at[pos], xb_in.at[pos], sxb.at[pos], rxb.at[pos], across)

    def zb(pos):
        return rcopy(
            zb_out.at[pos], zb_in.at[line], szb.at[pos], rzb.at[line], at(pos, side, head)
        )

    def add_heads(j):
        pos = places[j]
        hb(pos).wait_recv()
        xb_out[pos] = (
            own[j, far_side] + hb_in[pos, far_side].astype(jnp.float32)
        ).astype(jnp.bfloat16)
        xb(pos).start()

    def add_sides(j):
        pos = places[j]
        xb(pos).wait_recv()
        total = (
            own[j, side] + hb_in[pos, side].astype(jnp.float32)
            + xb_in[pos].astype(jnp.float32)
        )
        if j == 0:
            own[0, side] = total
        else:
            zb_out[pos] = total.astype(jnp.bfloat16)
            zb(pos).start()

    middle = low > 0
    for c in range(CHUNKS):
        x_arrive(0, c)
        if lines > 1:
            z_arrive(1, c)
    for j in range(1, lines):
        for c in range(CHUNKS):
            if j == 1 and lines > 2:
                z_arrive(2, c)
            if 2 < j + 1 < lines:

                @pl.when(jnp.logical_not(middle))
                def _():
                    z_arrive(j + 1, c)

            x_arrive(j, c)
            if 2 < j + 2 < lines:

                @pl.when(middle)
                def _():
                    z_arrive(j + 2, c)

        if j == 1:
            compute(0)
        compute(j)
        if j > 1:
            add_heads(j - 1)
        if j > 2:
            add_sides(j - 2)
    if lines > 1:
        add_heads(lines - 1)
    add_heads(0)
    if lines > 2:
        add_sides(lines - 2)
    if lines > 1:
        add_sides(lines - 1)
    add_sides(0)
    total = own[0, side]
    for j in range(1, lines):
        pos = places[j]
        rcopy(
            zb_out.at[pos], zb_in.at[pos], szb.at[pos], rzb.at[pos], across
        ).wait_recv()
        total += zb_in[pos].astype(jnp.float32)
    out[...] = total.astype(jnp.bfloat16)

    for step in range(1, experts):
        wt_send(step).wait_send()
    for j in range(lines):
        pos = places[j]
        for c in range(CHUNKS):

            @pl.when(jnp.logical_and(pos <= line, has_up))
            def _():
                z_send(pos, c, 0).wait_send()

            @pl.when(jnp.logical_and(pos >= line, has_down))
            def _():
                z_send(pos, c, 1).wait_send()

            x_send(pos, c).wait_send()
            h_send(pos, False, c).wait_send()
            h_send(pos, True, c).wait_send()
        hb(pos).wait_send()
        xb(pos).wait_send()
        if j > 0:
            zb(pos).wait_send()


def fused(tokens, expert_ids, gate_scores, gate_proj, up_proj, down_proj):
    experts = lax.axis_size("wide")
    lines = experts // 2
    rows, width = tokens.shape
    units, features = gate_proj.shape[1:]
    bf16, f32 = jnp.bfloat16, jnp.float32
    dma = pltpu.SemaphoreType.DMA
    vmem = pl.BlockSpec(memory_space=pltpu.VMEM)
    hbm = pl.BlockSpec(memory_space=pltpu.HBM)
    return pl.pallas_call(
        functools.partial(kernel, lines),
        out_shape=jax.ShapeDtypeStruct((rows, width), bf16),
        in_specs=[hbm, vmem, vmem, hbm, hbm, hbm],
        out_specs=vmem,
        scratch_shapes=[
            pltpu.VMEM((rows, width), bf16),
            pltpu.VMEM((units, features), bf16),
            pltpu.VMEM((units, features), bf16),
            pltpu.VMEM((units, features), bf16),
            pltpu.VMEM((lines, 2, 2, rows, width), bf16),
            pltpu.VMEM((experts, 128), f32),
            pltpu.VMEM((experts, experts, 128), f32),
            pltpu.VMEM((lines, 2, rows, width), bf16),
            pltpu.VMEM((lines, 2, rows, width), bf16),
            pltpu.VMEM((lines, 2, rows, width), f32),
            pltpu.VMEM((lines, rows, width), bf16),
            pltpu.VMEM((lines, rows, width), bf16),
            pltpu.VMEM((lines, rows, width), bf16),
            pltpu.VMEM((lines, rows, width), bf16),
            dma((4,)),
            dma((experts,)), dma((experts,)),
            dma((lines, CHUNKS, 2)), dma((lines, CHUNKS)),
            dma((lines, CHUNKS)), dma((lines, CHUNKS)),
            dma((lines, 2, CHUNKS)), dma((lines, 2, CHUNKS)),
            dma((lines,)), dma((lines,)),
            dma((lines,)), dma((lines,)),
            dma((lines,)), dma((lines,)),
        ],
        compiler_params=pltpu.CompilerParams(
            collective_id=0, has_side_effects=True, vmem_limit_bytes=63 * 1024 * 1024
        ),
    )(tokens, expert_ids.T, gate_scores.T, gate_proj, up_proj, down_proj)


def local(tokens, expert_ids, gate_scores, gate_proj, up_proj, down_proj):
    experts = lax.axis_size("wide")
    rows, width = tokens.shape
    everyone = expert_ids.shape[1] == experts and gate_proj.shape[0] == 1
    if everyone and experts % 2 == 0 and rows <= 128 and gate_proj.shape[2] == 2 * width:
        return fused(tokens, expert_ids, gate_scores, gate_proj, up_proj, down_proj)
    return spread(tokens, expert_ids, gate_scores, gate_proj, up_proj, down_proj)


def solution(mesh):
    return jax.shard_map(
        local,
        mesh=mesh,
        in_specs=(
            P(("groups", "wide"), "head"),
            P(("groups", "wide"), None),
            P(("groups", "wide"), None),
            P("wide", "head", None),
            P("wide", "head", None),
            P("wide", "head", None),
        ),
        out_specs=P(("groups", "wide"), "head"),
        check_vma=False,
    )
```

```python
import functools

import jax
import jax.numpy as jnp
from jax import lax
from jax.experimental import pallas as pl
from jax.experimental.pallas import tpu as pltpu
from jax.sharding import PartitionSpec as P


def spread(tokens, expert_ids, gate_scores, gate_proj, up_proj, down_proj):
    experts = lax.axis_size("wide")
    tok_rows, top_count = expert_ids.shape
    ceiling = (tok_rows * top_count + experts - 1) // experts
    capacity = min(tok_rows, max(2, tok_rows // 8, 2 * ceiling))
    flat_ids = expert_ids.reshape(-1)
    expert_numbers = jnp.arange(experts, dtype=jnp.int32)
    onehot = (flat_ids[:, None] == expert_numbers[None, :]).astype(jnp.int32)
    earlier = jnp.cumsum(onehot, axis=0) - onehot
    slot_index = jnp.sum(earlier * onehot, axis=1)
    position = flat_ids * capacity + slot_index
    targets = jnp.arange(experts * capacity, dtype=jnp.int32)
    placing = jnp.any(
        position.reshape(tok_rows, top_count)[:, :, None] == targets[None, None, :], axis=1
    ).astype(jnp.bfloat16)
    w_gate = gate_proj[0]
    w_up = up_proj[0]
    w_down = down_proj[0]
    placed = lax.dot_general(
        placing, tokens, (((0,), (0,)), ((), ())), preferred_element_type=jnp.float32
    )
    outgoing = placed.astype(jnp.bfloat16).reshape(experts, capacity, tokens.shape[1])
    full_rows = lax.all_gather(
        lax.all_to_all(outgoing, "wide", split_axis=0, concat_axis=0, tiled=True),
        "head",
        axis=2,
        tiled=True,
    )
    src_count, item_count, feature_width = full_rows.shape
    stacked = full_rows.reshape(src_count * item_count, feature_width)
    gate_part = lax.dot_general(
        stacked, w_gate, (((1,), (1,)), ((), ())), preferred_element_type=jnp.float32
    )
    up_part = lax.dot_general(
        stacked, w_up, (((1,), (1,)), ((), ())), preferred_element_type=jnp.float32
    )
    hidden = (jax.nn.silu(gate_part) * up_part).astype(jnp.bfloat16)
    partial_value = jnp.dot(hidden, w_down, preferred_element_type=jnp.float32)
    partial_value = partial_value.reshape(src_count, item_count, feature_width)
    back = lax.psum_scatter(
        partial_value.astype(jnp.bfloat16), "head", scatter_dimension=2, tiled=True
    ).astype(jnp.float32)
    returned = lax.all_to_all(
        back.astype(jnp.bfloat16), "wide", split_axis=0, concat_axis=0, tiled=True
    ).astype(back.dtype)
    picked = returned.reshape(experts * capacity, returned.shape[2])[position]
    picked = picked.reshape(tok_rows, top_count, returned.shape[2])
    mixed = jnp.sum(gate_scores[:, :, None] * picked, axis=1)
    return mixed.astype(jnp.bfloat16)


MESH = pl.DeviceIdType.MESH
CHUNKS = 2


def kernel(
    lines, tok_hbm, ids, scores, gate_hbm, up_hbm, down_hbm, out,
    tokens, w_gate, w_up, w_down, toks, wt_out, wt_in, hb_out, hb_in, own, xb_out, xb_in,
    zb_out, zb_in, load_sem, swz, rwz, swx, rwx, sz, rz, sx, rx, sh, rh, shb, rhb, sxb, rxb, szb, rzb,
):
    wide = lax.axis_index("wide")
    head = lax.axis_index("head")
    line = wide // 2
    side = wide % 2
    far_side = 1 - side
    other = 1 - head
    rows, width = tokens.shape
    experts = 2 * lines

    def at(line_to, side_to, head_to):
        return {"wide": line_to * 2 + side_to, "head": head_to}

    def rcopy(src, dst, ssem, rsem, target):
        return pltpu.make_async_remote_copy(
            src_ref=src, dst_ref=dst, send_sem=ssem, recv_sem=rsem,
            device_id=target, device_id_type=MESH,
        )

    partner = at(line, side, other)
    across = at(line, far_side, head)

    token_load = pltpu.make_async_copy(tok_hbm, tokens, load_sem.at[3])
    token_load.start()
    loads = [
        pltpu.make_async_copy(gate_hbm.at[0], w_gate, load_sem.at[0]),
        pltpu.make_async_copy(up_hbm.at[0], w_up, load_sem.at[1]),
        pltpu.make_async_copy(down_hbm.at[0], w_down, load_sem.at[2]),
    ]
    for c in loads:
        c.start()

    barrier = pltpu.get_barrier_semaphore()
    has_up = line < lines - 1
    has_down = line > 0

    @pl.when(has_up)
    def _():
        pl.semaphore_signal(
            barrier, inc=1, device_id=at(line + 1, side, head), device_id_type=MESH
        )

    @pl.when(has_down)
    def _():
        pl.semaphore_signal(
            barrier, inc=1, device_id=at(line - 1, side, head), device_id_type=MESH
        )

    pl.semaphore_signal(barrier, inc=1, device_id=across, device_id_type=MESH)
    pl.semaphore_signal(barrier, inc=1, device_id=partner, device_id_type=MESH)

    named = lax.broadcasted_iota(jnp.int32, (experts, rows), 0)
    turned = jnp.zeros((experts, rows), jnp.float32)
    for k in range(ids.shape[0]):
        turned += jnp.where(named == ids[k : k + 1], scores[k : k + 1], 0.0)
    turned = jnp.concatenate([turned, jnp.zeros((experts, 128 - rows), jnp.float32)], axis=1)
    wt_out[...] = turned
    wt_in[wide] = turned
    token_load.wait()
    toks[line, side, head] = tokens[...]
    pl.semaphore_wait(barrier, 2 + jnp.where(has_up, 1, 0) + jnp.where(has_down, 1, 0))

    chunk = rows // CHUNKS

    def cut(ref, c):
        return ref.at[pl.ds(c * chunk, chunk)]

    def slot(pos, sd, hf, c):
        return toks.at[pos, sd, hf, pl.ds(c * chunk, chunk)]

    def z_send(pos, c, way):
        src = cut(tokens, c) if pos is line else slot(pos, side, head, c)
        to = line + 1 - 2 * way
        return rcopy(
            src, slot(pos, side, head, c), sz.at[pos, c, way], rz.at[pos, c], at(to, side, head)
        )

    def x_send(pos, c):
        src = cut(tokens, c) if pos is line else slot(pos, side, head, c)
        return rcopy(src, slot(pos, side, head, c), sx.at[pos, c], rx.at[pos, c], across)

    def h_send(pos, far, c):
        sd = far_side if far else side
        src = cut(tokens, c) if pos is line and not far else slot(pos, sd, head, c)
        return rcopy(src, slot(pos, sd, head, c), sh.at[pos, sd, c], rh.at[pos, sd, c], partner)

    low = jnp.minimum(line, lines - 1 - line)
    up_is_long = line < lines - 1 - line
    toward = jnp.where(up_is_long, 1, -1)

    def order(j):
        d = (j + 1) // 2
        near = line + toward * d if j % 2 else line - toward * d
        return jnp.where(j <= 2 * low, near, jnp.where(up_is_long, j, lines - 1 - j))

    places = [line] + [order(j) for j in range(1, lines)]

    def wt_z(pos, way):
        src = wt_out if pos is line else wt_in.at[pos * 2 + side]
        to = line + 1 - 2 * way
        return rcopy(
            src, wt_in.at[pos * 2 + side], swz.at[pos, way], rwz.at[pos], at(to, side, head)
        )

    def wt_x(pos):
        src = wt_out if pos is line else wt_in.at[pos * 2 + side]
        return rcopy(src, wt_in.at[pos * 2 + side], swx.at[pos], rwx.at[pos], across)

    wt_x(line).start()

    @pl.when(has_up)
    def _():
        wt_z(line, 0).start()

    @pl.when(has_down)
    def _():
        wt_z(line, 1).start()

    for c in range(CHUNKS):
        x_send(line, c).start()

        @pl.when(has_up)
        def _():
            z_send(line, c, 0).start()

        @pl.when(has_down)
        def _():
            z_send(line, c, 1).start()

        h_send(line, False, c).start()

    def wt_arrive(j):
        pos = places[j]
        dst = wt_in.at[pos * 2 + side]
        rcopy(dst, dst, swz.at[pos, 0], rwz.at[pos], across).wait_recv()

        @pl.when(jnp.logical_and(pos < line, has_up))
        def _():
            wt_z(pos, 0).start()

        @pl.when(jnp.logical_and(pos > line, has_down))
        def _():
            wt_z(pos, 1).start()

        wt_x(pos).start()

    def z_arrive(j, c):
        pos = places[j]
        if c == 0:
            wt_arrive(j)
        dst = slot(pos, side, head, c)
        rcopy(dst, dst, sz.at[pos, c, 0], rz.at[pos, c], across).wait_recv()

        @pl.when(jnp.logical_and(pos < line, has_up))
        def _():
            z_send(pos, c, 0).start()

        @pl.when(jnp.logical_and(pos > line, has_down))
        def _():
            z_send(pos, c, 1).start()

        x_send(pos, c).start()
        h_send(pos, False, c).start()

    def x_arrive(j, c):
        pos = places[j]
        dst = slot(pos, far_side, head, c)
        rcopy(dst, dst, sx.at[pos, c], rx.at[pos, c], across).wait_recv()
        h_send(pos, True, c).start()

    mine = lax.broadcasted_iota(jnp.int32, (128, experts), 1) == wide

    def column(sender):
        return jnp.sum(
            jnp.where(mine, jnp.transpose(wt_in[sender]), 0.0), axis=1, keepdims=True
        )[:rows]

    nt = (((1,), (1,)), ((), ()))

    def compute(j):
        pos = places[j]
        for sd in range(2):
            for c in range(CHUNKS):
                dst = slot(pos, sd, other, c)
                rcopy(dst, dst, sh.at[pos, sd, c], rh.at[pos, sd, c], partner).wait_recv()
        if j == 0:
            loads[0].wait()
            loads[1].wait()
        dst = wt_in.at[pos * 2 + far_side]
        rcopy(dst, dst, swx.at[pos], rwx.at[pos], across).wait_recv()
        gate = jnp.zeros((2 * rows, w_gate.shape[0]), jnp.float32)
        up = gate
        for hf in range(2):
            block = toks[pos, :, hf].reshape(2 * rows, width)
            span = slice(hf * width, (hf + 1) * width)
            gate += lax.dot_general(block, w_gate[:, span], nt, preferred_element_type=jnp.float32)
            up += lax.dot_general(block, w_up[:, span], nt, preferred_element_type=jnp.float32)
        scale = jnp.concatenate([column(pos * 2), column(pos * 2 + 1)], axis=0)
        hidden = (gate / (1.0 + jnp.exp(-gate)) * up * scale).astype(jnp.bfloat16)
        if j == 0:
            loads[2].wait()
        theirs = pl.ds(pl.multiple_of(other * width, width), width)
        part = jnp.dot(hidden, w_down[:, theirs], preferred_element_type=jnp.float32)
        hb_out[pos] = part.astype(jnp.bfloat16).reshape(2, rows, width)
        hb(pos).start()
        ours = pl.ds(pl.multiple_of(head * width, width), width)
        part = jnp.dot(hidden, w_down[:, ours], preferred_element_type=jnp.float32)
        own[j] = part.reshape(2, rows, width)

    def hb(pos):
        return rcopy(hb_out.at[pos], hb_in.at[pos], shb.at[pos], rhb.at[pos], partner)

    def xb(pos, c):
        part = pl.ds(c * chunk, chunk)
        return rcopy(
            xb_out.at[pos, part], xb_in.at[pos, part], sxb.at[pos, c], rxb.at[pos, c], across
        )

    def zb(pos, c):
        part = pl.ds(c * chunk, chunk)
        return rcopy(
            zb_out.at[pos, part], zb_in.at[line, part], szb.at[pos, c], rzb.at[line, c],
            at(pos, side, head),
        )

    def add_heads(j):
        pos = places[j]
        hb(pos).wait_recv()
        for c in range(CHUNKS):
            part = slice(c * chunk, (c + 1) * chunk)
            xb_out[pos, part] = (
                own[j, far_side, part] + hb_in[pos, far_side, part].astype(jnp.float32)
            ).astype(jnp.bfloat16)
            xb(pos, c).start()

    def add_sides(j):
        pos = places[j]
        for c in range(CHUNKS):
            part = slice(c * chunk, (c + 1) * chunk)
            xb(pos, c).wait_recv()
            total = (
                own[j, side, part] + hb_in[pos, side, part].astype(jnp.float32)
                + xb_in[pos, part].astype(jnp.float32)
            )
            if j == 0:
                own[0, side, part] = total
            else:
                zb_out[pos, part] = total.astype(jnp.bfloat16)
                zb(pos, c).start()

    middle = low > 0

    def z_arrive_if(wanted, j):
        if j < lines:

            @pl.when(wanted)
            def _():
                for c in range(CHUNKS):
                    z_arrive(j, c)

    for c in range(CHUNKS):
        x_arrive(0, c)
        if lines > 1:
            z_arrive(1, c)
    z_arrive_if(middle, 2)
    compute(0)
    for j in range(1, lines):
        z_arrive_if(jnp.logical_not(middle), j + 1)
        for c in range(CHUNKS):
            x_arrive(j, c)
        z_arrive_if(middle, j + 2)
        if j > 1:
            add_heads(j - 1)
        compute(j)
        if j > 2:
            add_sides(j - 2)
    if lines > 1:
        add_heads(lines - 1)
    add_heads(0)
    if lines > 2:
        add_sides(lines - 2)
    if lines > 1:
        add_sides(lines - 1)
    add_sides(0)
    for j in range(1, lines):
        pos = places[j]
        for c in range(CHUNKS):
            part = pl.ds(c * chunk, chunk)
            dst = zb_in.at[pos, part]
            rcopy(dst, dst, szb.at[pos, c], rzb.at[pos, c], across).wait_recv()
            total = own[0, side, c * chunk : (c + 1) * chunk] + zb_in[pos, c * chunk : (c + 1) * chunk].astype(jnp.float32)
            if j == lines - 1:
                out[c * chunk : (c + 1) * chunk] = total.astype(jnp.bfloat16)
            else:
                own[0, side, c * chunk : (c + 1) * chunk] = total

    for j in range(lines):
        pos = places[j]
        for c in range(CHUNKS):

            @pl.when(jnp.logical_and(pos <= line, has_up))
            def _():
                z_send(pos, c, 0).wait_send()

            @pl.when(jnp.logical_and(pos >= line, has_down))
            def _():
                z_send(pos, c, 1).wait_send()

            x_send(pos, c).wait_send()
            h_send(pos, False, c).wait_send()
            h_send(pos, True, c).wait_send()
        @pl.when(jnp.logical_and(pos <= line, has_up))
        def _():
            wt_z(pos, 0).wait_send()

        @pl.when(jnp.logical_and(pos >= line, has_down))
        def _():
            wt_z(pos, 1).wait_send()

        wt_x(pos).wait_send()
        hb(pos).wait_send()
        for c in range(CHUNKS):
            xb(pos, c).wait_send()
            if j > 0:
                zb(pos, c).wait_send()


def fused(tokens, expert_ids, gate_scores, gate_proj, up_proj, down_proj):
    experts = lax.axis_size("wide")
    lines = experts // 2
    rows, width = tokens.shape
    units, features = gate_proj.shape[1:]
    bf16, f32 = jnp.bfloat16, jnp.float32
    dma = pltpu.SemaphoreType.DMA
    vmem = pl.BlockSpec(memory_space=pltpu.VMEM)
    hbm = pl.BlockSpec(memory_space=pltpu.HBM)
    return pl.pallas_call(
        functools.partial(kernel, lines),
        out_shape=jax.ShapeDtypeStruct((rows, width), bf16),
        in_specs=[hbm, vmem, vmem, hbm, hbm, hbm],
        out_specs=vmem,
        scratch_shapes=[
            pltpu.VMEM((rows, width), bf16),
            pltpu.VMEM((units, features), bf16),
            pltpu.VMEM((units, features), bf16),
            pltpu.VMEM((units, features), bf16),
            pltpu.VMEM((lines, 2, 2, rows, width), bf16),
            pltpu.VMEM((experts, 128), f32),
            pltpu.VMEM((experts, experts, 128), f32),
            pltpu.VMEM((lines, 2, rows, width), bf16),
            pltpu.VMEM((lines, 2, rows, width), bf16),
            pltpu.VMEM((lines, 2, rows, width), f32),
            pltpu.VMEM((lines, rows, width), bf16),
            pltpu.VMEM((lines, rows, width), bf16),
            pltpu.VMEM((lines, rows, width), bf16),
            pltpu.VMEM((lines, rows, width), bf16),
            dma((4,)),
            dma((lines, 2)), dma((lines,)),
            dma((lines,)), dma((lines,)),
            dma((lines, CHUNKS, 2)), dma((lines, CHUNKS)),
            dma((lines, CHUNKS)), dma((lines, CHUNKS)),
            dma((lines, 2, CHUNKS)), dma((lines, 2, CHUNKS)),
            dma((lines,)), dma((lines,)),
            dma((lines, CHUNKS)), dma((lines, CHUNKS)),
            dma((lines, CHUNKS)), dma((lines, CHUNKS)),
        ],
        compiler_params=pltpu.CompilerParams(
            collective_id=0, has_side_effects=True, vmem_limit_bytes=63 * 1024 * 1024
        ),
    )(tokens, expert_ids.T, gate_scores.T, gate_proj, up_proj, down_proj)


def local(tokens, expert_ids, gate_scores, gate_proj, up_proj, down_proj):
    experts = lax.axis_size("wide")
    rows, width = tokens.shape
    everyone = expert_ids.shape[1] == experts and gate_proj.shape[0] == 1
    if everyone and experts % 2 == 0 and rows <= 128 and gate_proj.shape[2] == 2 * width:
        return fused(tokens, expert_ids, gate_scores, gate_proj, up_proj, down_proj)
    return spread(tokens, expert_ids, gate_scores, gate_proj, up_proj, down_proj)


def solution(mesh):
    return jax.shard_map(
        local,
        mesh=mesh,
        in_specs=(
            P(("groups", "wide"), "head"),
            P(("groups", "wide"), None),
            P(("groups", "wide"), None),
            P("wide", "head", None),
            P("wide", "head", None),
            P("wide", "head", None),
        ),
        out_specs=P(("groups", "wide"), "head"),
        check_vma=False,
    )
```

```python
import functools

import jax
import jax.numpy as jnp
from jax import lax
from jax.experimental import pallas as pl
from jax.experimental.pallas import tpu as pltpu
from jax.sharding import PartitionSpec as P


def spread(tokens, expert_ids, gate_scores, gate_proj, up_proj, down_proj):
    experts = lax.axis_size("wide")
    tok_rows, top_count = expert_ids.shape
    ceiling = (tok_rows * top_count + experts - 1) // experts
    capacity = min(tok_rows, max(2, tok_rows // 8, 2 * ceiling))
    flat_ids = expert_ids.reshape(-1)
    expert_numbers = jnp.arange(experts, dtype=jnp.int32)
    onehot = (flat_ids[:, None] == expert_numbers[None, :]).astype(jnp.int32)
    earlier = jnp.cumsum(onehot, axis=0) - onehot
    slot_index = jnp.sum(earlier * onehot, axis=1)
    position = flat_ids * capacity + slot_index
    targets = jnp.arange(experts * capacity, dtype=jnp.int32)
    placing = jnp.any(
        position.reshape(tok_rows, top_count)[:, :, None] == targets[None, None, :], axis=1
    ).astype(jnp.bfloat16)
    w_gate = gate_proj[0]
    w_up = up_proj[0]
    w_down = down_proj[0]
    placed = lax.dot_general(
        placing, tokens, (((0,), (0,)), ((), ())), preferred_element_type=jnp.float32
    )
    outgoing = placed.astype(jnp.bfloat16).reshape(experts, capacity, tokens.shape[1])
    full_rows = lax.all_gather(
        lax.all_to_all(outgoing, "wide", split_axis=0, concat_axis=0, tiled=True),
        "head",
        axis=2,
        tiled=True,
    )
    src_count, item_count, feature_width = full_rows.shape
    stacked = full_rows.reshape(src_count * item_count, feature_width)
    gate_part = lax.dot_general(
        stacked, w_gate, (((1,), (1,)), ((), ())), preferred_element_type=jnp.float32
    )
    up_part = lax.dot_general(
        stacked, w_up, (((1,), (1,)), ((), ())), preferred_element_type=jnp.float32
    )
    hidden = (jax.nn.silu(gate_part) * up_part).astype(jnp.bfloat16)
    partial_value = jnp.dot(hidden, w_down, preferred_element_type=jnp.float32)
    partial_value = partial_value.reshape(src_count, item_count, feature_width)
    back = lax.psum_scatter(
        partial_value.astype(jnp.bfloat16), "head", scatter_dimension=2, tiled=True
    ).astype(jnp.float32)
    returned = lax.all_to_all(
        back.astype(jnp.bfloat16), "wide", split_axis=0, concat_axis=0, tiled=True
    ).astype(back.dtype)
    picked = returned.reshape(experts * capacity, returned.shape[2])[position]
    picked = picked.reshape(tok_rows, top_count, returned.shape[2])
    mixed = jnp.sum(gate_scores[:, :, None] * picked, axis=1)
    return mixed.astype(jnp.bfloat16)


MESH = pl.DeviceIdType.MESH
CHUNKS = 2


def kernel(
    lines, tok_hbm, ids, scores, gate_hbm, up_hbm, down_hbm, out,
    tokens, w_gate, w_up, w_down, toks, wt_out, wt_in, hb_out, hb_in, own, xb_out, xb_in,
    zb_out, zb_in, load_sem, swz, rwz, swx, rwx, sz, rz, sx, rx, sh, rh, shb, rhb, sxb, rxb, szb, rzb,
):
    wide = lax.axis_index("wide")
    head = lax.axis_index("head")
    line = wide // 2
    side = wide % 2
    far_side = 1 - side
    other = 1 - head
    rows, width = tokens.shape
    experts = 2 * lines

    def at(line_to, side_to, head_to):
        return {"wide": line_to * 2 + side_to, "head": head_to}

    def rcopy(src, dst, ssem, rsem, target):
        return pltpu.make_async_remote_copy(
            src_ref=src, dst_ref=dst, send_sem=ssem, recv_sem=rsem,
            device_id=target, device_id_type=MESH,
        )

    partner = at(line, side, other)
    across = at(line, far_side, head)

    token_load = pltpu.make_async_copy(tok_hbm, tokens, load_sem.at[3])
    token_load.start()
    loads = [
        pltpu.make_async_copy(gate_hbm.at[0], w_gate, load_sem.at[0]),
        pltpu.make_async_copy(up_hbm.at[0], w_up, load_sem.at[1]),
        pltpu.make_async_copy(down_hbm.at[0], w_down, load_sem.at[2]),
    ]
    for c in loads:
        c.start()

    barrier = pltpu.get_barrier_semaphore()
    has_up = line < lines - 1
    has_down = line > 0

    @pl.when(has_up)
    def _():
        pl.semaphore_signal(
            barrier, inc=1, device_id=at(line + 1, side, head), device_id_type=MESH
        )

    @pl.when(has_down)
    def _():
        pl.semaphore_signal(
            barrier, inc=1, device_id=at(line - 1, side, head), device_id_type=MESH
        )

    pl.semaphore_signal(barrier, inc=1, device_id=across, device_id_type=MESH)
    pl.semaphore_signal(barrier, inc=1, device_id=partner, device_id_type=MESH)

    named = lax.broadcasted_iota(jnp.int32, (experts, rows), 0)
    turned = jnp.zeros((experts, rows), jnp.float32)
    for k in range(ids.shape[0]):
        turned += jnp.where(named == ids[k : k + 1], scores[k : k + 1], 0.0)
    turned = jnp.concatenate([turned, jnp.zeros((experts, 128 - rows), jnp.float32)], axis=1)
    wt_out[...] = turned
    wt_in[wide] = turned
    token_load.wait()
    toks[line, side, head] = tokens[...]
    pl.semaphore_wait(barrier, 2 + jnp.where(has_up, 1, 0) + jnp.where(has_down, 1, 0))

    chunk = rows // CHUNKS

    def cut(ref, c):
        return ref.at[pl.ds(c * chunk, chunk)]

    def slot(pos, sd, hf, c):
        return toks.at[pos, sd, hf, pl.ds(c * chunk, chunk)]

    def z_send(pos, c, way):
        src = cut(tokens, c) if pos is line else slot(pos, side, head, c)
        to = line + 1 - 2 * way
        return rcopy(
            src, slot(pos, side, head, c), sz.at[pos, c, way], rz.at[pos, c], at(to, side, head)
        )

    def x_send(pos, c):
        src = cut(tokens, c) if pos is line else slot(pos, side, head, c)
        return rcopy(src, slot(pos, side, head, c), sx.at[pos, c], rx.at[pos, c], across)

    def h_send(pos, far, c):
        sd = far_side if far else side
        src = cut(tokens, c) if pos is line and not far else slot(pos, sd, head, c)
        return rcopy(src, slot(pos, sd, head, c), sh.at[pos, sd, c], rh.at[pos, sd, c], partner)

    low = jnp.minimum(line, lines - 1 - line)
    up_is_long = line < lines - 1 - line
    toward = jnp.where(up_is_long, 1, -1)

    def order(j):
        d = (j + 1) // 2
        near = line + toward * d if j % 2 else line - toward * d
        return jnp.where(j <= 2 * low, near, jnp.where(up_is_long, j, lines - 1 - j))

    places = [line] + [order(j) for j in range(1, lines)]

    def wt_z(pos, way):
        src = wt_out if pos is line else wt_in.at[pos * 2 + side]
        to = line + 1 - 2 * way
        return rcopy(
            src, wt_in.at[pos * 2 + side], swz.at[pos, way], rwz.at[pos], at(to, side, head)
        )

    def wt_x(pos):
        src = wt_out if pos is line else wt_in.at[pos * 2 + side]
        return rcopy(src, wt_in.at[pos * 2 + side], swx.at[pos], rwx.at[pos], across)

    wt_x(line).start()

    @pl.when(has_up)
    def _():
        wt_z(line, 0).start()

    @pl.when(has_down)
    def _():
        wt_z(line, 1).start()

    for c in range(CHUNKS):
        x_send(line, c).start()

        @pl.when(has_up)
        def _():
            z_send(line, c, 0).start()

        @pl.when(has_down)
        def _():
            z_send(line, c, 1).start()

        h_send(line, False, c).start()

    def wt_arrive(j):
        pos = places[j]
        dst = wt_in.at[pos * 2 + side]
        rcopy(dst, dst, swz.at[pos, 0], rwz.at[pos], across).wait_recv()

        @pl.when(jnp.logical_and(pos < line, has_up))
        def _():
            wt_z(pos, 0).start()

        @pl.when(jnp.logical_and(pos > line, has_down))
        def _():
            wt_z(pos, 1).start()

        wt_x(pos).start()

    def z_arrive(j, c):
        pos = places[j]
        if c == 0:
            wt_arrive(j)
        dst = slot(pos, side, head, c)
        rcopy(dst, dst, sz.at[pos, c, 0], rz.at[pos, c], across).wait_recv()

        @pl.when(jnp.logical_and(pos < line, has_up))
        def _():
            z_send(pos, c, 0).start()

        @pl.when(jnp.logical_and(pos > line, has_down))
        def _():
            z_send(pos, c, 1).start()

        x_send(pos, c).start()
        h_send(pos, False, c).start()

    def x_arrive(j, c):
        pos = places[j]
        dst = slot(pos, far_side, head, c)
        rcopy(dst, dst, sx.at[pos, c], rx.at[pos, c], across).wait_recv()
        h_send(pos, True, c).start()

    mine = lax.broadcasted_iota(jnp.int32, (128, experts), 1) == wide

    def column(sender):
        return jnp.sum(
            jnp.where(mine, jnp.transpose(wt_in[sender]), 0.0), axis=1, keepdims=True
        )[:rows]

    nt = (((1,), (1,)), ((), ()))

    def compute(j):
        pos = places[j]
        for sd in range(2):
            for c in range(CHUNKS):
                dst = slot(pos, sd, other, c)
                rcopy(dst, dst, sh.at[pos, sd, c], rh.at[pos, sd, c], partner).wait_recv()
        if j == 0:
            loads[0].wait()
            loads[1].wait()
        dst = wt_in.at[pos * 2 + far_side]
        rcopy(dst, dst, swx.at[pos], rwx.at[pos], across).wait_recv()
        gate = jnp.zeros((2 * rows, w_gate.shape[0]), jnp.float32)
        up = gate
        for hf in range(2):
            block = toks[pos, :, hf].reshape(2 * rows, width)
            span = slice(hf * width, (hf + 1) * width)
            gate += lax.dot_general(block, w_gate[:, span], nt, preferred_element_type=jnp.float32)
            up += lax.dot_general(block, w_up[:, span], nt, preferred_element_type=jnp.float32)
        scale = jnp.concatenate([column(pos * 2), column(pos * 2 + 1)], axis=0)
        hidden = (gate / (1.0 + jnp.exp(-gate)) * up * scale).astype(jnp.bfloat16)
        if j == 0:
            loads[2].wait()
        theirs = pl.ds(pl.multiple_of(other * width, width), width)
        part = jnp.dot(hidden, w_down[:, theirs], preferred_element_type=jnp.float32)
        hb_out[pos] = part.astype(jnp.bfloat16).reshape(2, rows, width)
        hb(pos).start()
        ours = pl.ds(pl.multiple_of(head * width, width), width)
        part = jnp.dot(hidden, w_down[:, ours], preferred_element_type=jnp.float32)
        own[j] = part.reshape(2, rows, width)

    def hb(pos):
        return rcopy(hb_out.at[pos], hb_in.at[pos], shb.at[pos], rhb.at[pos], partner)

    def xb(pos, c):
        part = pl.ds(c * chunk, chunk)
        return rcopy(
            xb_out.at[pos, part], xb_in.at[pos, part], sxb.at[pos, c], rxb.at[pos, c], across
        )

    def zb(pos, c):
        part = pl.ds(c * chunk, chunk)
        return rcopy(
            zb_out.at[pos, part], zb_in.at[line, part], szb.at[pos, c], rzb.at[line, c],
            at(pos, side, head),
        )

    def add_heads(j):
        pos = places[j]
        hb(pos).wait_recv()
        for c in range(CHUNKS):
            part = slice(c * chunk, (c + 1) * chunk)
            xb_out[pos, part] = (
                own[j, far_side, part] + hb_in[pos, far_side, part].astype(jnp.float32)
            ).astype(jnp.bfloat16)
            xb(pos, c).start()

    def add_sides(j):
        pos = places[j]
        for c in range(CHUNKS):
            part = slice(c * chunk, (c + 1) * chunk)
            xb(pos, c).wait_recv()
            total = (
                own[j, side, part] + hb_in[pos, side, part].astype(jnp.float32)
                + xb_in[pos, part].astype(jnp.float32)
            )
            if j == 0:
                own[0, side, part] = total
            else:
                zb_out[pos, part] = total.astype(jnp.bfloat16)
                zb(pos, c).start()

    middle = low > 0

    def z_arrive_if(wanted, j):
        if j < lines:

            @pl.when(wanted)
            def _():
                for c in range(CHUNKS):
                    z_arrive(j, c)

    for c in range(CHUNKS):
        x_arrive(0, c)
        if lines > 1:
            z_arrive(1, c)
    z_arrive_if(middle, 2)
    compute(0)
    for j in range(1, lines):
        z_arrive_if(jnp.logical_not(middle), j + 1)
        for c in range(CHUNKS):
            x_arrive(j, c)
        z_arrive_if(middle, j + 2)
        if j > 1:
            add_heads(j - 1)
        compute(j)
    if lines > 1:
        add_heads(lines - 1)
    add_heads(0)
    for j in range(1, lines - 2):
        add_sides(j)
    if lines > 2:
        add_sides(lines - 2)
    if lines > 1:
        add_sides(lines - 1)
    add_sides(0)
    for j in range(1, lines):
        pos = places[j]
        for c in range(CHUNKS):
            part = pl.ds(c * chunk, chunk)
            dst = zb_in.at[pos, part]
            rcopy(dst, dst, szb.at[pos, c], rzb.at[pos, c], across).wait_recv()
            total = own[0, side, c * chunk : (c + 1) * chunk] + zb_in[pos, c * chunk : (c + 1) * chunk].astype(jnp.float32)
            if j == lines - 1:
                out[c * chunk : (c + 1) * chunk] = total.astype(jnp.bfloat16)
            else:
                own[0, side, c * chunk : (c + 1) * chunk] = total

    for j in range(lines):
        pos = places[j]
        for c in range(CHUNKS):

            @pl.when(jnp.logical_and(pos <= line, has_up))
            def _():
                z_send(pos, c, 0).wait_send()

            @pl.when(jnp.logical_and(pos >= line, has_down))
            def _():
                z_send(pos, c, 1).wait_send()

            x_send(pos, c).wait_send()
            h_send(pos, False, c).wait_send()
            h_send(pos, True, c).wait_send()
        @pl.when(jnp.logical_and(pos <= line, has_up))
        def _():
            wt_z(pos, 0).wait_send()

        @pl.when(jnp.logical_and(pos >= line, has_down))
        def _():
            wt_z(pos, 1).wait_send()

        wt_x(pos).wait_send()
        hb(pos).wait_send()
        for c in range(CHUNKS):
            xb(pos, c).wait_send()
            if j > 0:
                zb(pos, c).wait_send()


def fused(tokens, expert_ids, gate_scores, gate_proj, up_proj, down_proj):
    experts = lax.axis_size("wide")
    lines = experts // 2
    rows, width = tokens.shape
    units, features = gate_proj.shape[1:]
    bf16, f32 = jnp.bfloat16, jnp.float32
    dma = pltpu.SemaphoreType.DMA
    vmem = pl.BlockSpec(memory_space=pltpu.VMEM)
    hbm = pl.BlockSpec(memory_space=pltpu.HBM)
    return pl.pallas_call(
        functools.partial(kernel, lines),
        out_shape=jax.ShapeDtypeStruct((rows, width), bf16),
        in_specs=[hbm, vmem, vmem, hbm, hbm, hbm],
        out_specs=vmem,
        scratch_shapes=[
            pltpu.VMEM((rows, width), bf16),
            pltpu.VMEM((units, features), bf16),
            pltpu.VMEM((units, features), bf16),
            pltpu.VMEM((units, features), bf16),
            pltpu.VMEM((lines, 2, 2, rows, width), bf16),
            pltpu.VMEM((experts, 128), f32),
            pltpu.VMEM((experts, experts, 128), f32),
            pltpu.VMEM((lines, 2, rows, width), bf16),
            pltpu.VMEM((lines, 2, rows, width), bf16),
            pltpu.VMEM((lines, 2, rows, width), f32),
            pltpu.VMEM((lines, rows, width), bf16),
            pltpu.VMEM((lines, rows, width), bf16),
            pltpu.VMEM((lines, rows, width), bf16),
            pltpu.VMEM((lines, rows, width), bf16),
            dma((4,)),
            dma((lines, 2)), dma((lines,)),
            dma((lines,)), dma((lines,)),
            dma((lines, CHUNKS, 2)), dma((lines, CHUNKS)),
            dma((lines, CHUNKS)), dma((lines, CHUNKS)),
            dma((lines, 2, CHUNKS)), dma((lines, 2, CHUNKS)),
            dma((lines,)), dma((lines,)),
            dma((lines, CHUNKS)), dma((lines, CHUNKS)),
            dma((lines, CHUNKS)), dma((lines, CHUNKS)),
        ],
        compiler_params=pltpu.CompilerParams(
            collective_id=0, has_side_effects=True, vmem_limit_bytes=63 * 1024 * 1024
        ),
    )(tokens, expert_ids.T, gate_scores.T, gate_proj, up_proj, down_proj)


def local(tokens, expert_ids, gate_scores, gate_proj, up_proj, down_proj):
    experts = lax.axis_size("wide")
    rows, width = tokens.shape
    everyone = expert_ids.shape[1] == experts and gate_proj.shape[0] == 1
    if everyone and experts % 2 == 0 and rows <= 128 and gate_proj.shape[2] == 2 * width:
        return fused(tokens, expert_ids, gate_scores, gate_proj, up_proj, down_proj)
    return spread(tokens, expert_ids, gate_scores, gate_proj, up_proj, down_proj)


def solution(mesh):
    return jax.shard_map(
        local,
        mesh=mesh,
        in_specs=(
            P(("groups", "wide"), "head"),
            P(("groups", "wide"), None),
            P(("groups", "wide"), None),
            P("wide", "head", None),
            P("wide", "head", None),
            P("wide", "head", None),
        ),
        out_specs=P(("groups", "wide"), "head"),
        check_vma=False,
    )
```
